32 devices in a mesh: lat: 4 (over y, x), lev: 8 (over z, core).
Axes of the slice: x: 2, y: 2, z: 4, core: 2. Of those that a mesh axis runs over, the one named last changes fastest.
Arguments:
- state: float32 [6, 12, 32, 1152], P(None, 'lat', 'lev'), may hold values from -6 to 6
- courant: float32 [2, 12, 32, 1152], P(None, 'lat', 'lev'), may hold values from -0.4 to 0.4
- offsets: int32 [2, 12, 32, 1152], P(None, 'lat', 'lev'), may hold values from -1 to 2
- log_thickness: float32 [12, 32, 1152], P('lat', 'lev'), may hold values from 0.05 to 0.5
- surface: float32 [12, 1152], P('lat'), may hold values from -6 to 6
- remap_level: int32 [12, 32, 1152], P('lat', None, 'lev'), may hold values from 0 to 31, as said below
- remap_weight: float32 [12, 32, 1152], P('lat', None, 'lev'), may hold values from 0 to 1
Outputs:
- remapped: float32 [6, 12, 32, 1152], P(None, 'lat', 'lev')
- geopotential: float32 [12, 32, 1152], P('lat', 'lev')
The draws below stay inside these ranges and needn't reach their ends.
Inputs may be any that keep to these rules, and one draw needn't show every extreme that they name: `remap_level`: the source level of target level k lies within 2 of k.
All inputs are finite; a program needn't handle non-finite values.
Results may differ from the reference program's by a relative error of at most 0.00007.
Values sent between devices are 32-bit elements; how exact they have to be, the bound alone decides.
A program may use at most 64 MiB of HBM per device.

```python
import math
import jax
import jax.numpy as jnp
from jax import lax

NLON = 1152
SUBSTEPS = 2
FIELDS = 6
NLAT = 12
LEV = 32


def draw_remap_level(key, part):
    spread = jax.random.randint(key, (NLAT, LEV, NLON), -2, 3, dtype=jnp.int32)
    levels = jnp.arange(LEV, dtype=jnp.int32)[None, :, None]
    return jnp.clip(levels + spread, 0, LEV - 1).astype(jnp.int32)


def place_ends(array, stream_key, least, top_value):
    extent = array.shape
    index_at = [jax.random.randint(jax.random.fold_in(stream_key, axis), (), 0, extent[axis]) for axis in range(len(extent))]
    array = array.at[tuple(index_at)].set(least)
    longest = extent.index(max(extent))
    index_at[longest] = (index_at[longest] + 1) % extent[longest]
    return array.at[tuple(index_at)].set(top_value)


def level_of(own_key, extent, shards, smallest, largest):
    def one(axis_at, shards_of):
        steps = jax.random.uniform(jax.random.fold_in(jax.random.fold_in(own_key, 6), axis_at), (shards_of,), jnp.float32, smallest / len(shards), largest / len(shards))
        return jnp.repeat(jnp.exp(steps), extent[axis_at] // shards_of).reshape((-1,) + (1,) * (len(extent) - axis_at - 1))

    factor_of = one(*shards[0])
    for cut in shards[1:]:
        factor_of = factor_of * one(*cut)
    return factor_of


def gaussian(stream_key, shape, scale, most, pieces=(), kind=jnp.bfloat16):
    result = jax.random.normal(stream_key, shape, jnp.float32) * scale
    if len(pieces) > 0:
        result = level_of(stream_key, shape, pieces, -0.22, 0.18) * result
    return jnp.clip(result, min=-most, max=most).astype(kind)


def setup_inputs(seed: int = 0) -> dict:
    key_list = jax.random.split(jax.random.key(seed), 8)
    state = gaussian(key_list[0], (FIELDS, NLAT, LEV, NLON), 1.0, 6.0, ((1, 4), (2, 8)), jnp.float32)
    courant = jnp.clip(jax.random.uniform(key_list[1], (2, NLAT, LEV, NLON), jnp.float32, -0.4, 0.4) * level_of(key_list[1], (2, NLAT, LEV, NLON), ((1, 4), (2, 8)), -0.4, 0.0), -0.4, 0.4)
    offsets = place_ends(jax.random.randint(key_list[2], (2, NLAT, LEV, NLON), -1, 3), jax.random.fold_in(key_list[2], 1), -1, 2).astype(jnp.int32)
    log_thickness = jnp.clip(jnp.exp(math.log(0.5) - 2.3025851 * jax.random.uniform(key_list[3], (NLAT, LEV, NLON), jnp.float32) ** level_of(key_list[3], (NLAT, LEV, NLON), ((0, 4), (1, 8)), -0.2, 0.2)), 0.05, 0.5)
    surface = gaussian(key_list[4], (NLAT, NLON), 1.0, 6.0, ((0, 4),), jnp.float32)
    remap_level = draw_remap_level(jax.random.fold_in(key_list[7], 71), 0)
    remap_weight = jnp.clip(1.0 * jax.random.uniform(key_list[6], (NLAT, LEV, NLON), jnp.float32) ** level_of(key_list[6], (NLAT, LEV, NLON), ((0, 4), (2, 8)), -0.2, 0.2), 0.0, 1.0)
    return {"state": state, "courant": courant, "offsets": offsets, "log_thickness": log_thickness, "surface": surface, "remap_level": remap_level, "remap_weight": remap_weight}


def parabola(q, source, weight):
    n = q.shape[-2]
    widths = [(0, 0)] * (q.ndim - 2) + [(2, 2), (0, 0)]
    padded = jnp.pad(q, widths, mode="edge")
    edges = (7.0 * (padded[..., 1:n + 2, :] + padded[..., 2:n + 3, :]) - (padded[..., 0:n + 1, :] + padded[..., 3:n + 4, :])) / 12.0
    centre = jnp.take_along_axis(q, source, axis=-2)
    left = jnp.take_along_axis(edges[..., :n, :], source, axis=-2)
    right = jnp.take_along_axis(edges[..., 1:, :], source, axis=-2)
    slope = right - left
    curve = 6.0 * centre - 3.0 * (left + right)
    return left + weight * (slope + curve * (1.0 - weight))


def reference(state, courant, offsets, log_thickness, surface, remap_level, remap_weight):
    rows = state.shape[1]
    width = state.shape[3]
    row_index = jnp.arange(rows, dtype=jnp.int32)[:, None, None]
    north_index = row_index + offsets[0] + 2
    east_index = (jnp.arange(width, dtype=jnp.int32)[None, None, :] + offsets[1]) % width

    def advect(q):
        for substep in range(SUBSTEPS):
            padded = jnp.pad(q, ((2, 2), (0, 0), (0, 0)))
            north = courant[0] * jnp.take_along_axis(padded, north_index, axis=0)
            south = jnp.concatenate([jnp.zeros_like(north[:1]), north[:-1]], axis=0)
            east = courant[1] * jnp.take_along_axis(q, east_index, axis=2)
            west = jnp.roll(east, 1, axis=2)
            q = q - (north - south) - (east - west)
        return q

    advected = lax.map(advect, state)
    heating = advected[0] * log_thickness
    lower = jnp.cumsum(heating[:, ::-1], axis=1)[:, ::-1] - heating
    geopotential = surface[:, None, :] + lower + 0.5 * heating
    remapped = lax.map(lambda q: parabola(q, remap_level, remap_weight), advected)
    return remapped, geopotential
```

```python
import functools

import jax
import jax.numpy as jnp
from jax import lax
from jax.experimental import pallas as pl
from jax.experimental.pallas import tpu as pltpu
from jax.sharding import PartitionSpec as P

SUBSTEPS = 2


def extended_2(block, sides, width):
    for axis, dim in sides:
        count = lax.axis_size(axis)
        forward = [(i, i + 1) for i in range(count - 1)]
        backward = [(target, source) for source, target in forward]
        low = lax.ppermute(
            lax.slice_in_dim(block, block.shape[dim] - width, None, axis=dim), axis, forward
        )
        high = lax.ppermute(lax.slice_in_dim(block, 0, width, axis=dim), axis, backward)
        block = jnp.concatenate([low, block, high], axis=dim)
    return block


def from_behind(x, axis, by):
    count = lax.axis_size(axis)
    pairs = [(i, i + by) for i in range(count) if 0 <= i + by < count]
    return lax.ppermute(x, axis, pairs)


def entering(x, axis, combine, identity):
    count, position = (lax.axis_size(axis), lax.axis_index(axis))
    everything = lax.all_gather(x, axis)
    start = jnp.broadcast_to(jnp.asarray(identity, x.dtype), x.shape)

    def lap(k, before):
        at = count - 1 - k
        reached = at > position
        new = combine(before, everything[at])
        return jnp.where(reached, new, before)

    return lax.fori_loop(0, count, lap, start)


def local_parabola(extended, delta, weight):
    margin = 4
    count = extended.shape[-2] - 2 * margin
    edges = (
        7.0 * (extended[..., 1:-2, :] + extended[..., 2:-1, :])
        - (extended[..., :-3, :] + extended[..., 3:, :])
    ) / 12.0
    centre = jnp.zeros(extended.shape[:-2] + (count, extended.shape[-1]), jnp.float32)
    left = centre
    right = centre
    for offset in range(-2, 3):
        chosen = delta == offset
        start = margin + offset
        centre = jnp.where(chosen, extended[..., start : start + count, :], centre)
        left = jnp.where(chosen, edges[..., start - 2 : start - 2 + count, :], left)
        right = jnp.where(chosen, edges[..., start - 1 : start - 1 + count, :], right)
    slope = right - left
    curve = 6.0 * centre - 3.0 * (left + right)
    return left + weight * (slope + curve * (1.0 - weight))


def add_terms(earlier, later):
    return earlier + later


def per_device(state, courant, offsets, log_thickness, surface, remap_level, remap_weight):
    count, rows, levels, width = state.shape
    north_masks = [offsets[0] == offset for offset in range(-1, 3)]
    east_masks = [offsets[1] == offset for offset in range(-1, 3)]
    field = state
    for substep in range(SUBSTEPS):
        padded = extended_2(field, (("lat", 1),), 2)
        picked = jnp.zeros_like(field)
        for number, offset in enumerate(range(-1, 3)):
            picked = jnp.where(
                north_masks[number][None], padded[:, offset + 2 : offset + 2 + rows], picked
            )
        north = courant[0][None] * picked
        below = from_behind(north[:, rows - 1 :], "lat", 1)
        south = jnp.concatenate([below, north[:, : rows - 1]], axis=1)
        moved = jnp.zeros_like(field)
        for number, offset in enumerate(range(-1, 3)):
            moved = jnp.where(east_masks[number][None], jnp.roll(field, -offset, axis=3), moved)
        east = courant[1][None] * moved
        west = jnp.roll(east, 1, axis=3)
        field = field - (north - south) - (east - west)
    heating = field[0] * log_thickness
    lower_local = jnp.cumsum(heating[:, ::-1], axis=1)[:, ::-1] - heating
    column_sum = jnp.sum(heating, axis=1)
    deeper = entering(column_sum, "lev", add_terms, jnp.zeros_like(column_sum))
    geopotential = surface[:, None, :] + deeper[:, None, :] + lower_local + 0.5 * heating
    total_levels = remap_level.shape[1]
    delta_col = (remap_level - jnp.arange(total_levels, dtype=jnp.int32)[None, :, None]).astype(
        jnp.float32
    )
    inputs = lax.all_to_all(
        jnp.stack([delta_col, remap_weight]), "lev", split_axis=2, concat_axis=3, tiled=True
    )
    margin = 4
    before = []
    before.insert(0, from_behind(field, "lev", 1))
    after_list = [from_behind(field, "lev", -1)]
    joined = jnp.concatenate(before + [field] + after_list, axis=2)
    first = lax.axis_index("lev") * levels
    whole = levels * lax.axis_size("lev")
    position = first - margin + jnp.arange(levels + 2 * margin, dtype=jnp.int32)
    where_from = jnp.clip(position, 0, whole - 1) - (first - margin)
    extended = jnp.take(joined, where_from, axis=2)
    remapped = local_parabola(extended, inputs[0][None], inputs[1][None])
    return (remapped, geopotential)


MARGIN = 4
MESH = pl.DeviceIdType.MESH


def remote(src, dst, send, recv, axis, peer):
    return pltpu.make_async_remote_copy(
        src_ref=src,
        dst_ref=dst,
        send_sem=send,
        recv_sem=recv,
        device_id={axis: peer},
        device_id_type=MESH,
    )


def kernel(
    lats,
    levs,
    chunks,
    state,
    courant,
    offsets,
    thickness,
    surface,
    remap_level,
    remap_weight,
    out,
    geo,
    pack,
    pack_off,
    work,
    work_off,
    mid,
    ret,
    ext,
    rpack,
    rrecv,
    rall,
    hsum,
    sums,
    deep,
    fs,
    fr,
    gs,
    gr,
    bs,
    br,
    zs,
    zr,
    rs,
    rr,
    ss,
    sr,
):
    count, rows, levels, width = state.shape
    slab = rows * lats
    piece = remap_level.shape[2]
    span = width // chunks
    me = lax.axis_index("lat")
    lev = lax.axis_index("lev")

    barrier = pltpu.get_barrier_semaphore()
    for d in range(1, lats):
        pl.semaphore_signal(
            barrier, inc=1, device_id={"lat": lax.rem(me + d, lats)}, device_id_type=MESH
        )
    for d in range(1, levs):
        pl.semaphore_signal(
            barrier, inc=1, device_id={"lev": lax.rem(lev + d, levs)}, device_id_type=MESH
        )

    def pack_level(level):
        at = pl.ds(level, 1)
        for r in range(rows):
            for f in range(count):
                pack[level, r, f : f + 1, :] = state[f, r, at, :]
            for f in range(2):
                pack[level, r, count + f : count + f + 1, :] = courant[f, r, at, :]
                pack_off[level, r, f : f + 1, :] = offsets[f, r, at, :]

    fwd = []
    for d in range(1, lats):
        peer = lax.rem(me + d, lats)
        pack_level(peer)
        if d == 1:
            pl.semaphore_wait(barrier, lats + levs - 2)
        a = remote(
            pack.at[peer], work.at[pl.ds(2 + rows * me, rows)], fs.at[d], fr.at[d], "lat", peer
        )
        b = remote(
            pack_off.at[peer], work_off.at[pl.ds(1 + rows * me, rows)], gs.at[d], gr.at[d], "lat", peer
        )
        a.start()
        b.start()
        fwd += [a, b]

    first = []
    for p in range(levs):
        for r in range(rows):
            lo = p * levels
            ks = lo + lax.broadcasted_iota(jnp.int32, (levels, piece), 0)
            rpack[p, 0, r] = (remap_level[r, lo : lo + levels, :] - ks).astype(jnp.float32)
            rpack[p, 1, r] = remap_weight[r, lo : lo + levels, :]
    for d in range(1, levs):
        peer = lax.rem(lev + d, levs)
        c = remote(rpack.at[peer], rrecv.at[lev], rs.at[d], rr.at[d], "lev", peer)
        c.start()
        first.append(c)
    rrecv[lev] = rpack[lev]

    pack_level(me)
    for r in range(rows):
        work[2 + rows * me + r] = pack[me, r]
        work_off[1 + rows * me + r] = pack_off[me, r]
    blank = jnp.zeros(work.shape[1:], jnp.float32)
    for r in (0, 1, slab + 2, slab + 3):
        work[r] = blank
        mid[r] = blank

    for c in fwd:
        c.wait_recv()

    whole = work.shape[1:]

    def substep(source, store):
        def face(j, south):
            q = source[j + 2]
            o0 = jnp.broadcast_to(work_off[j + 1, 0:1, :], whole)
            o1 = jnp.broadcast_to(work_off[j + 1, 1:2, :], whole)
            c0 = jnp.broadcast_to(work[j + 2, count : count + 1, :], whole)
            c1 = jnp.broadcast_to(work[j + 2, count + 1 : count + 2, :], whole)
            up = jnp.where(
                o0 <= 0,
                jnp.where(o0 == 0, q, source[j + 1]),
                jnp.where(o0 == 1, source[j + 3], source[j + 4]),
            )
            north = c0 * up
            side = jnp.where(
                o1 <= 0,
                jnp.where(o1 == 0, q, pltpu.roll(q, 1, 1)),
                jnp.where(o1 == 1, pltpu.roll(q, width - 1, 1), pltpu.roll(q, width - 2, 1)),
            )
            east = c1 * side
            west = pltpu.roll(east, 1, 1)
            store(j, q - (north - south) - (east - west))
            return north

        lax.fori_loop(0, slab, face, jnp.zeros(whole, jnp.float32))

    def store_mid(j, value):
        mid[j + 2] = value

    def store_ret(j, value):
        ret[j] = value[:count]

    substep(work, store_mid)
    substep(mid, store_ret)

    back = []
    for n in range(chunks):
        lanes = pl.ds(n * span, span)
        some = []
        for d in range(1, lats):
            peer = lax.rem(me + d, lats)
            c = remote(
                ret.at[pl.ds(rows * peer, rows), :, lanes],
                ext.at[MARGIN + me, :, :, lanes],
                bs.at[n, d],
                br.at[n, d],
                "lat",
                peer,
            )
            c.start()
            some.append(c)
        back.append(some)
    for r in range(rows):
        ext[MARGIN + me, r] = ret[rows * me + r]
    for c in first:
        c.wait_recv()
    for p in range(levs):
        rall[:, :, :, p * piece : (p + 1) * piece] = rrecv[p]

    def up_copy(n):
        lanes = pl.ds(n * span, span)
        return remote(
            ext.at[pl.ds(levels, MARGIN), :, :, lanes],
            ext.at[pl.ds(0, MARGIN), :, :, lanes],
            zs.at[n, 0],
            zr.at[n, 0],
            "lev",
            jnp.minimum(lev + 1, levs - 1),
        )

    def down_copy(n):
        lanes = pl.ds(n * span, span)
        return remote(
            ext.at[pl.ds(MARGIN, MARGIN), :, :, lanes],
            ext.at[pl.ds(MARGIN + levels, MARGIN), :, :, lanes],
            zs.at[n, 1],
            zr.at[n, 1],
            "lev",
            jnp.maximum(lev - 1, 0),
        )

    def sum_copy(n, d):
        return remote(
            hsum.at[n], sums.at[n, d], ss.at[n, d], sr.at[n, d], "lev", jnp.maximum(lev - d, 0)
        )

    def heating(n, r):
        lanes = pl.ds(n * span, span)
        return [
            ext[MARGIN + k, r, 0:1, lanes] * thickness[r, k : k + 1, lanes]
            for k in range(levels)
        ]

    for n in range(chunks):
        lanes = pl.ds(n * span, span)
        for c in back[n]:
            c.wait_recv()

        @pl.when(lev < levs - 1)
        def _():
            up_copy(n).start()

        @pl.when(lev > 0)
        def _():
            down_copy(n).start()

        for r in range(rows):
            heat = heating(n, r)
            hsum[n, r : r + 1, :] = functools.reduce(add_terms, heat)
        for d in range(1, levs):

            @pl.when(lev >= d)
            def _():
                sum_copy(n, d).start()

    for n in range(chunks):
        lanes = pl.ds(n * span, span)

        @pl.when(lev > 0)
        def _():
            up_copy(n).wait_recv()

        @pl.when(lev < levs - 1)
        def _():
            down_copy(n).wait_recv()

        @pl.when(lev == 0)
        def _():
            for m in range(MARGIN):
                ext[m, :, :, lanes] = ext[MARGIN, :, :, lanes]

        @pl.when(lev == levs - 1)
        def _():
            for m in range(MARGIN):
                ext[MARGIN + levels + m, :, :, lanes] = ext[MARGIN + levels - 1, :, :, lanes]

        for r in range(rows):
            q = [ext[m, r, :, lanes] for m in range(levels + 2 * MARGIN)]
            edge = {
                m: (7.0 * (q[m - 1] + q[m]) - (q[m - 2] + q[m + 1])) * (1.0 / 12.0)
                for m in range(2, levels + 2 * MARGIN - 1)
            }
            results = []
            for k in range(levels):
                delta = jnp.broadcast_to(rall[0, r, k : k + 1, lanes], q[0].shape)
                weight = jnp.broadcast_to(rall[1, r, k : k + 1, lanes], q[0].shape)
                s = k + MARGIN
                centre, left, right = q[s - 2], edge[s - 2], edge[s - 1]
                for o in range(-1, 3):
                    chosen = delta == float(o)
                    centre = jnp.where(chosen, q[s + o], centre)
                    left = jnp.where(chosen, edge[s + o], left)
                    right = jnp.where(chosen, edge[s + o + 1], right)
                curve = 6.0 * centre - 3.0 * (left + right)
                value = left + weight * ((right - left) + curve * (1.0 - weight))
                for f in range(count):
                    out[f, r, k : k + 1, lanes] = value[f : f + 1]

        deep[...] = jnp.zeros_like(deep)
        for d in range(1, levs):

            @pl.when(lev + d < levs)
            def _():
                sum_copy(n, d).wait_recv()
                deep[...] += sums[n, d]

        for r in range(rows):
            heat = heating(n, r)
            below = surface[r : r + 1, lanes] + deep[r : r + 1, :]
            for k in range(levels - 1, -1, -1):
                geo[r, k : k + 1, lanes] = below + 0.5 * heat[k]
                below = below + heat[k]

    for c in fwd + first:
        c.wait_send()
    for n in range(chunks):
        for c in back[n]:
            c.wait_send()

        @pl.when(lev < levs - 1)
        def _():
            up_copy(n).wait_send()

        @pl.when(lev > 0)
        def _():
            down_copy(n).wait_send()

        for d in range(1, levs):

            @pl.when(lev >= d)
            def _():
                sum_copy(n, d).wait_send()


def fused(lats, levs, chunks, state, courant, offsets, thickness, surface, level, weight):
    count, rows, levels, width = state.shape
    piece = level.shape[2]
    slab = rows * lats
    span = width // chunks
    f32 = jnp.float32
    dma = pltpu.SemaphoreType.DMA
    vmem = pl.BlockSpec(memory_space=pltpu.VMEM)
    return pl.pallas_call(
        functools.partial(kernel, lats, levs, chunks),
        out_shape=(
            jax.ShapeDtypeStruct(state.shape, f32),
            jax.ShapeDtypeStruct(thickness.shape, f32),
        ),
        in_specs=[vmem] * 7,
        out_specs=(vmem, vmem),
        scratch_shapes=[
            pltpu.VMEM((levels, rows, count + 2, width), f32),
            pltpu.VMEM((levels, rows, 2, width), jnp.int32),
            pltpu.VMEM((slab + 4, count + 2, width), f32),
            pltpu.VMEM((slab + 2, 2, width), jnp.int32),
            pltpu.VMEM((slab + 4, count + 2, width), f32),
            pltpu.VMEM((slab, count, width), f32),
            pltpu.VMEM((levels + 2 * MARGIN, rows, count, width), f32),
            pltpu.VMEM((levs, 2, rows, levels, piece), f32),
            pltpu.VMEM((levs, 2, rows, levels, piece), f32),
            pltpu.VMEM((2, rows, levels, width), f32),
            pltpu.VMEM((chunks, rows, span), f32),
            pltpu.VMEM((chunks, levs, rows, span), f32),
            pltpu.VMEM((rows, span), f32),
            dma((lats,)),
            dma((lats,)),
            dma((lats,)),
            dma((lats,)),
            dma((chunks, lats)),
            dma((chunks, lats)),
            dma((chunks, 2)),
            dma((chunks, 2)),
            dma((levs,)),
            dma((levs,)),
            dma((chunks, levs)),
            dma((chunks, levs)),
        ],
        compiler_params=pltpu.CompilerParams(collective_id=0, has_side_effects=True),
    )(state, courant, offsets, thickness, surface, level, weight)


def solution(mesh):
    in_specs = (
        P(None, "lat", "lev", None),
        P(None, "lat", "lev", None),
        P(None, "lat", "lev", None),
        P("lat", "lev", None),
        P("lat", None),
        P("lat", None, "lev"),
        P("lat", None, "lev"),
    )
    out_specs = (P(None, "lat", "lev", None), P("lat", "lev", None))
    lats, levs = mesh.shape["lat"], mesh.shape["lev"]

    def body(state, *rest):
        levels, width = state.shape[2:]
        chunks = next((c for c in (3, 2, 1) if width % (c * 128) == 0), 0)
        if levels != lats or levels < MARGIN or chunks == 0 or levs < 2:
            return per_device(state, *rest)
        return fused(lats, levs, chunks, state, *rest)

    return jax.shard_map(
        body, mesh=mesh, in_specs=in_specs, out_specs=out_specs, check_vma=False
    )
```

```python
import functools

import jax
import jax.numpy as jnp
from jax import lax
from jax.experimental import pallas as pl
from jax.experimental.pallas import tpu as pltpu
from jax.sharding import PartitionSpec as P

SUBSTEPS = 2


def extended_2(block, sides, width):
    for axis, dim in sides:
        count = lax.axis_size(axis)
        forward = [(i, i + 1) for i in range(count - 1)]
        backward = [(target, source) for source, target in forward]
        low = lax.ppermute(
            lax.slice_in_dim(block, block.shape[dim] - width, None, axis=dim), axis, forward
        )
        high = lax.ppermute(lax.slice_in_dim(block, 0, width, axis=dim), axis, backward)
        block = jnp.concatenate([low, block, high], axis=dim)
    return block


def from_behind(x, axis, by):
    count = lax.axis_size(axis)
    pairs = [(i, i + by) for i in range(count) if 0 <= i + by < count]
    return lax.ppermute(x, axis, pairs)


def entering(x, axis, combine, identity):
    count, position = (lax.axis_size(axis), lax.axis_index(axis))
    everything = lax.all_gather(x, axis)
    start = jnp.broadcast_to(jnp.asarray(identity, x.dtype), x.shape)

    def lap(k, before):
        at = count - 1 - k
        reached = at > position
        new = combine(before, everything[at])
        return jnp.where(reached, new, before)

    return lax.fori_loop(0, count, lap, start)


def local_parabola(extended, delta, weight):
    margin = 4
    count = extended.shape[-2] - 2 * margin
    edges = (
        7.0 * (extended[..., 1:-2, :] + extended[..., 2:-1, :])
        - (extended[..., :-3, :] + extended[..., 3:, :])
    ) / 12.0
    centre = jnp.zeros(extended.shape[:-2] + (count, extended.shape[-1]), jnp.float32)
    left = centre
    right = centre
    for offset in range(-2, 3):
        chosen = delta == offset
        start = margin + offset
        centre = jnp.where(chosen, extended[..., start : start + count, :], centre)
        left = jnp.where(chosen, edges[..., start - 2 : start - 2 + count, :], left)
        right = jnp.where(chosen, edges[..., start - 1 : start - 1 + count, :], right)
    slope = right - left
    curve = 6.0 * centre - 3.0 * (left + right)
    return left + weight * (slope + curve * (1.0 - weight))


def add_terms(earlier, later):
    return earlier + later


def per_device(state, courant, offsets, log_thickness, surface, remap_level, remap_weight):
    count, rows, levels, width = state.shape
    north_masks = [offsets[0] == offset for offset in range(-1, 3)]
    east_masks = [offsets[1] == offset for offset in range(-1, 3)]
    field = state
    for substep in range(SUBSTEPS):
        padded = extended_2(field, (("lat", 1),), 2)
        picked = jnp.zeros_like(field)
        for number, offset in enumerate(range(-1, 3)):
            picked = jnp.where(
                north_masks[number][None], padded[:, offset + 2 : offset + 2 + rows], picked
            )
        north = courant[0][None] * picked
        below = from_behind(north[:, rows - 1 :], "lat", 1)
        south = jnp.concatenate([below, north[:, : rows - 1]], axis=1)
        moved = jnp.zeros_like(field)
        for number, offset in enumerate(range(-1, 3)):
            moved = jnp.where(east_masks[number][None], jnp.roll(field, -offset, axis=3), moved)
        east = courant[1][None] * moved
        west = jnp.roll(east, 1, axis=3)
        field = field - (north - south) - (east - west)
    heating = field[0] * log_thickness
    lower_local = jnp.cumsum(heating[:, ::-1], axis=1)[:, ::-1] - heating
    column_sum = jnp.sum(heating, axis=1)
    deeper = entering(column_sum, "lev", add_terms, jnp.zeros_like(column_sum))
    geopotential = surface[:, None, :] + deeper[:, None, :] + lower_local + 0.5 * heating
    total_levels = remap_level.shape[1]
    delta_col = (remap_level - jnp.arange(total_levels, dtype=jnp.int32)[None, :, None]).astype(
        jnp.float32
    )
    inputs = lax.all_to_all(
        jnp.stack([delta_col, remap_weight]), "lev", split_axis=2, concat_axis=3, tiled=True
    )
    margin = 4
    before = []
    before.insert(0, from_behind(field, "lev", 1))
    after_list = [from_behind(field, "lev", -1)]
    joined = jnp.concatenate(before + [field] + after_list, axis=2)
    first = lax.axis_index("lev") * levels
    whole = levels * lax.axis_size("lev")
    position = first - margin + jnp.arange(levels + 2 * margin, dtype=jnp.int32)
    where_from = jnp.clip(position, 0, whole - 1) - (first - margin)
    extended = jnp.take(joined, where_from, axis=2)
    remapped = local_parabola(extended, inputs[0][None], inputs[1][None])
    return (remapped, geopotential)


MARGIN = 4
UNROLL = 3
MESH = pl.DeviceIdType.MESH


def remote(src, dst, send, recv, axis, peer):
    return pltpu.make_async_remote_copy(
        src_ref=src,
        dst_ref=dst,
        send_sem=send,
        recv_sem=recv,
        device_id={axis: peer},
        device_id_type=MESH,
    )


def compact(count):
    sizes, size = [8] * (count // 8), 4
    count %= 8
    while count:
        if count >= size:
            sizes.append(size)
            count -= size
        size //= 2
    return sizes


def kernel(lats, levs, chunks, *refs):
    (
        h_state,
        h_courant,
        h_offsets,
        h_thickness,
        h_surface,
        h_level,
        h_weight,
        out,
        geo,
        state,
        courant,
        offsets,
        thickness,
        surface,
        remap_level,
        remap_weight,
        pack,
        pack_off,
        work,
        work_off,
        mid,
        rpack,
        rrecv,
        rall,
        hsum,
        psum,
        csum,
        sums,
        deep,
        ins,
        fs,
        fr,
        gs,
        gr,
        bs,
        br,
        zs,
        zr,
        rs,
        rr,
        ps,
        pr,
        ss,
        sr,
    ) = refs[:44]
    count, rows, levels, width = state.shape
    groups = compact(count)
    parts = len(groups)
    rets, exts = refs[44 : 44 + parts], refs[44 + parts :]
    slab = rows * lats
    piece = remap_level.shape[2]
    span = width // chunks
    me = lax.axis_index("lat")
    lev = lax.axis_index("lev")
    core = lax.rem(lev, 2)

    loads = [
        pltpu.make_async_copy(a, b, ins.at[n])
        for n, (a, b) in enumerate(
            (
                (h_state, state),
                (h_courant, courant),
                (h_offsets, offsets),
                (h_level, remap_level),
                (h_weight, remap_weight),
                (h_thickness, thickness),
                (h_surface, surface),
            )
        )
    ]
    for c in loads:
        c.start()
    barrier = pltpu.get_barrier_semaphore()
    for d in range(1, levs):
        pl.semaphore_signal(
            barrier, inc=1, device_id={"lev": lax.rem(lev + d, levs)}, device_id_type=MESH
        )
    for d in range(1, lats):
        pl.semaphore_signal(
            barrier, inc=1, device_id={"lat": lax.rem(me + d, lats)}, device_id_type=MESH
        )
    for c in loads[:3]:
        c.wait()
    for level in range(levels):
        at = slice(level, level + 1)
        for r in range(rows):
            for f in range(count):
                pack[level, r, f : f + 1, :] = state[f, r, at, :]
            for f in range(2):
                pack[level, r, count + f : count + f + 1, :] = courant[f, r, at, :]
                pack_off[level, r, f : f + 1, :] = offsets[f, r, at, :]

    pl.semaphore_wait(barrier, lats + levs - 2)
    fwd = []
    for d in range(1, lats):
        peer = lax.rem(me + d, lats)
        a = remote(
            pack.at[peer], work.at[pl.ds(2 + rows * me, rows)], fs.at[d], fr.at[d], "lat", peer
        )
        b = remote(
            pack_off.at[peer], work_off.at[pl.ds(1 + rows * me, rows)], gs.at[d], gr.at[d], "lat", peer
        )
        a.start()
        b.start()
        fwd += [a, b]

    for c in loads[3:]:
        c.wait()
    first = []
    for p in range(levs):
        for r in range(rows):
            lo = p * levels
            ks = lo + lax.broadcasted_iota(jnp.int32, (levels, piece), 0)
            rpack[p, 0, r] = (remap_level[r, lo : lo + levels, :] - ks).astype(jnp.float32)
            rpack[p, 1, r] = remap_weight[r, lo : lo + levels, :]
    for d in range(1, levs):
        peer = lax.rem(lev + d, levs)
        c = remote(rpack.at[peer], rrecv.at[lev], rs.at[d], rr.at[d], "lev", peer)
        c.start()
        first.append(c)
    rrecv[lev] = rpack[lev]

    for r in range(rows):
        work[2 + rows * me + r] = pack[me, r]
        work_off[1 + rows * me + r] = pack_off[me, r]
    blank = jnp.zeros(work.shape[1:], jnp.float32)
    for r in (0, 1, slab + 2, slab + 3):
        work[r] = blank
        mid[r] = blank

    for c in fwd:
        c.wait_recv()

    whole = work.shape[1:]

    def substep(source, store):
        def face(j, south):
            q = source[j + 2]
            o0 = jnp.broadcast_to(work_off[j + 1, 0:1, :], whole)
            o1 = jnp.broadcast_to(work_off[j + 1, 1:2, :], whole)
            c0 = jnp.broadcast_to(work[j + 2, count : count + 1, :], whole)
            c1 = jnp.broadcast_to(work[j + 2, count + 1 : count + 2, :], whole)
            up = jnp.where(
                o0 <= 0,
                jnp.where(o0 == 0, q, source[j + 1]),
                jnp.where(o0 == 1, source[j + 3], source[j + 4]),
            )
            north = c0 * up
            side = jnp.where(
                o1 <= 0,
                jnp.where(o1 == 0, q, pltpu.roll(q, 1, 1)),
                jnp.where(o1 == 1, pltpu.roll(q, width - 1, 1), pltpu.roll(q, width - 2, 1)),
            )
            east = c1 * side
            west = pltpu.roll(east, 1, 1)
            store(j, q - (north - south) - (east - west))
            return north

        lax.fori_loop(0, slab, face, jnp.zeros(whole, jnp.float32), unroll=UNROLL)

    def store_mid(j, value):
        mid[j + 2] = value

    def store_ret(j, value):
        lo = 0
        for ref, size in zip(rets, groups):
            ref[j] = value[lo : lo + size]
            lo += size

    substep(work, store_mid)
    substep(mid, store_ret)

    back = []
    for n in range(chunks):
        lanes = pl.ds(n * span, span)
        some = []
        for d in range(1, lats):
            peer = lax.rem(me + d, lats)
            for g in range(parts):
                c = remote(
                    rets[g].at[pl.ds(rows * peer, rows), :, lanes],
                    exts[g].at[MARGIN + me, :, :, lanes],
                    bs.at[n, d, g],
                    br.at[n, d, g],
                    "lat",
                    peer,
                )
                c.start()
                some.append(c)
        back.append(some)
    for r in range(rows):
        for ret, ext in zip(rets, exts):
            ext[MARGIN + me, r] = ret[rows * me + r]
    for c in first:
        c.wait_recv()
    for p in range(levs):
        rall[:, :, :, p * piece : (p + 1) * piece] = rrecv[p]

    def level_copies(n, way):
        lanes = pl.ds(n * span, span)
        source, target = ((levels, 0), (MARGIN, MARGIN + levels))[way]
        peer = (jnp.minimum(lev + 1, levs - 1), jnp.maximum(lev - 1, 0))[way]
        return [
            remote(
                exts[g].at[pl.ds(source, MARGIN), :, :, lanes],
                exts[g].at[pl.ds(target, MARGIN), :, :, lanes],
                zs.at[n, way, g],
                zr.at[n, way, g],
                "lev",
                peer,
            )
            for g in range(parts)
        ]

    def pair_copy(n):
        return remote(hsum.at[n], psum.at[n], ps.at[n], pr.at[n], "lev", lev + 1 - 2 * core)

    def sum_copy(n, d):
        return remote(
            csum.at[n], sums.at[n, d], ss.at[n, d], sr.at[n, d], "lev", jnp.maximum(lev - 2 * d, core)
        )

    def heating(n, r):
        lanes = pl.ds(n * span, span)
        return [
            exts[0][MARGIN + k, r, 0:1, lanes] * thickness[r, k : k + 1, lanes]
            for k in range(levels)
        ]

    def pass_on(n):
        pair_copy(n).wait_recv()
        csum[n] = hsum[n] + psum[n]
        for d in range(1, levs // 2):

            @pl.when(lev >= 2 * d)
            def _():
                sum_copy(n, d).start()

    for n in range(chunks):
        lanes = pl.ds(n * span, span)
        for c in back[n]:
            c.wait_recv()
        for r in range(rows):
            hsum[n, r] = functools.reduce(add_terms, heating(n, r))
        pair_copy(n).start()

        @pl.when(lev < levs - 1)
        def _():
            for c in level_copies(n, 0):
                c.start()

        @pl.when(lev > 0)
        def _():
            for c in level_copies(n, 1):
                c.start()

        if n > 0:
            pass_on(n - 1)
    pass_on(chunks - 1)

    for n in range(chunks):
        lanes = pl.ds(n * span, span)

        @pl.when(lev > 0)
        def _():
            for c in level_copies(n, 0):
                c.wait_recv()

        @pl.when(lev < levs - 1)
        def _():
            for c in level_copies(n, 1):
                c.wait_recv()

        @pl.when(lev == 0)
        def _():
            for ext in exts:
                for m in range(MARGIN):
                    ext[m, :, :, lanes] = ext[MARGIN, :, :, lanes]

        @pl.when(lev == levs - 1)
        def _():
            for ext in exts:
                for m in range(MARGIN):
                    ext[MARGIN + levels + m, :, :, lanes] = ext[MARGIN + levels - 1, :, :, lanes]

        for r in range(rows):
            lo = 0
            for ext, size in zip(exts, groups):
                q = [ext[m, r, :, lanes] for m in range(levels + 2 * MARGIN)]
                edge = {
                    m: (7.0 * (q[m - 1] + q[m]) - (q[m - 2] + q[m + 1])) * (1.0 / 12.0)
                    for m in range(2, levels + 2 * MARGIN - 1)
                }
                for k in range(levels):
                    delta = jnp.broadcast_to(rall[0, r, k : k + 1, lanes], q[0].shape)
                    weight = jnp.broadcast_to(rall[1, r, k : k + 1, lanes], q[0].shape)
                    s = k + MARGIN
                    centre, left, right = q[s - 2], edge[s - 2], edge[s - 1]
                    for o in range(-1, 3):
                        chosen = delta == float(o)
                        centre = jnp.where(chosen, q[s + o], centre)
                        left = jnp.where(chosen, edge[s + o], left)
                        right = jnp.where(chosen, edge[s + o + 1], right)
                    curve = 6.0 * centre - 3.0 * (left + right)
                    value = left + weight * ((right - left) + curve * (1.0 - weight))
                    for f in range(size):
                        out[lo + f, r, k : k + 1, lanes] = value[f : f + 1]
                lo += size

    for n in range(chunks):
        lanes = pl.ds(n * span, span)
        deep[...] = jnp.where(core == 0, psum[n], jnp.zeros_like(deep))
        for d in range(1, levs // 2):

            @pl.when(lev + 2 * d < levs)
            def _():
                sum_copy(n, d).wait_recv()
                deep[...] += sums[n, d]

        for r in range(rows):
            heat = heating(n, r)
            below = surface[r : r + 1, lanes] + deep[r]
            for k in range(levels - 1, -1, -1):
                geo[r, k : k + 1, lanes] = below + 0.5 * heat[k]
                below = below + heat[k]

    for c in fwd + first:
        c.wait_send()
    for n in range(chunks):
        for c in back[n]:
            c.wait_send()
        pair_copy(n).wait_send()

        @pl.when(lev < levs - 1)
        def _():
            for c in level_copies(n, 0):
                c.wait_send()

        @pl.when(lev > 0)
        def _():
            for c in level_copies(n, 1):
                c.wait_send()

        for d in range(1, levs // 2):

            @pl.when(lev >= 2 * d)
            def _():
                sum_copy(n, d).wait_send()


def fused(lats, levs, chunks, *args):
    state, courant, offsets, thickness, surface, level, weight = args
    count, rows, levels, width = state.shape
    piece = level.shape[2]
    slab = rows * lats
    span = width // chunks
    f32 = jnp.float32
    dma = pltpu.SemaphoreType.DMA
    groups = compact(count)
    parts = len(groups)
    return pl.pallas_call(
        functools.partial(kernel, lats, levs, chunks),
        out_shape=(pltpu.VMEM(state.shape, f32), pltpu.VMEM(thickness.shape, f32)),
        in_specs=[pl.BlockSpec(memory_space=pl.ANY)] * 7,
        scratch_shapes=[
            *(pltpu.VMEM(x.shape, x.dtype) for x in args),
            pltpu.VMEM((levels, rows, count + 2, width), f32),
            pltpu.VMEM((levels, rows, 2, width), jnp.int32),
            pltpu.VMEM((slab + 4, count + 2, width), f32),
            pltpu.VMEM((slab + 2, 2, width), jnp.int32),
            pltpu.VMEM((slab + 4, count + 2, width), f32),
            pltpu.VMEM((levs, 2, rows, levels, piece), f32),
            pltpu.VMEM((levs, 2, rows, levels, piece), f32),
            pltpu.VMEM((2, rows, levels, width), f32),
            pltpu.VMEM((chunks, rows, 1, span), f32),
            pltpu.VMEM((chunks, rows, 1, span), f32),
            pltpu.VMEM((chunks, rows, 1, span), f32),
            pltpu.VMEM((chunks, levs // 2, rows, 1, span), f32),
            pltpu.VMEM((rows, 1, span), f32),
            dma((7,)),
            dma((lats,)),
            dma((lats,)),
            dma((lats,)),
            dma((lats,)),
            dma((chunks, lats, parts)),
            dma((chunks, lats, parts)),
            dma((chunks, 2, parts)),
            dma((chunks, 2, parts)),
            dma((levs,)),
            dma((levs,)),
            dma((chunks,)),
            dma((chunks,)),
            dma((chunks, levs // 2)),
            dma((chunks, levs // 2)),
            *(pltpu.VMEM((slab, g, width), f32) for g in groups),
            *(pltpu.VMEM((levels + 2 * MARGIN, rows, g, width), f32) for g in groups),
        ],
        compiler_params=pltpu.CompilerParams(collective_id=0, has_side_effects=True),
    )(*args)


def solution(mesh):
    in_specs = (
        P(None, "lat", "lev", None),
        P(None, "lat", "lev", None),
        P(None, "lat", "lev", None),
        P("lat", "lev", None),
        P("lat", None),
        P("lat", None, "lev"),
        P("lat", None, "lev"),
    )
    out_specs = (P(None, "lat", "lev", None), P("lat", "lev", None))
    lats, levs = mesh.shape["lat"], mesh.shape["lev"]

    def body(state, *rest):
        levels, width = state.shape[2:]
        chunks = next((c for c in (3, 2, 1) if width % (c * 128) == 0), 0)
        if levels != lats or levels < MARGIN or chunks == 0 or levs % 2:
            return per_device(state, *rest)
        return fused(lats, levs, chunks, state, *rest)

    return jax.shard_map(
        body, mesh=mesh, in_specs=in_specs, out_specs=out_specs, check_vma=False
    )
```

```python
import functools

import jax
import jax.numpy as jnp
from jax import lax
from jax.experimental import pallas as pl
from jax.experimental.pallas import tpu as pltpu
from jax.sharding import PartitionSpec as P

SUBSTEPS = 2


def extended_2(block, sides, width):
    for axis, dim in sides:
        count = lax.axis_size(axis)
        forward = [(i, i + 1) for i in range(count - 1)]
        backward = [(target, source) for source, target in forward]
        low = lax.ppermute(
            lax.slice_in_dim(block, block.shape[dim] - width, None, axis=dim), axis, forward
        )
        high = lax.ppermute(lax.slice_in_dim(block, 0, width, axis=dim), axis, backward)
        block = jnp.concatenate([low, block, high], axis=dim)
    return block


def from_behind(x, axis, by):
    count = lax.axis_size(axis)
    pairs = [(i, i + by) for i in range(count) if 0 <= i + by < count]
    return lax.ppermute(x, axis, pairs)


def entering(x, axis, combine, identity):
    count, position = (lax.axis_size(axis), lax.axis_index(axis))
    everything = lax.all_gather(x, axis)
    start = jnp.broadcast_to(jnp.asarray(identity, x.dtype), x.shape)

    def lap(k, before):
        at = count - 1 - k
        reached = at > position
        new = combine(before, everything[at])
        return jnp.where(reached, new, before)

    return lax.fori_loop(0, count, lap, start)


def local_parabola(extended, delta, weight):
    margin = 4
    count = extended.shape[-2] - 2 * margin
    edges = (
        7.0 * (extended[..., 1:-2, :] + extended[..., 2:-1, :])
        - (extended[..., :-3, :] + extended[..., 3:, :])
    ) / 12.0
    centre = jnp.zeros(extended.shape[:-2] + (count, extended.shape[-1]), jnp.float32)
    left = centre
    right = centre
    for offset in range(-2, 3):
        chosen = delta == offset
        start = margin + offset
        centre = jnp.where(chosen, extended[..., start : start + count, :], centre)
        left = jnp.where(chosen, edges[..., start - 2 : start - 2 + count, :], left)
        right = jnp.where(chosen, edges[..., start - 1 : start - 1 + count, :], right)
    slope = right - left
    curve = 6.0 * centre - 3.0 * (left + right)
    return left + weight * (slope + curve * (1.0 - weight))


def add_terms(earlier, later):
    return earlier + later


def per_device(state, courant, offsets, log_thickness, surface, remap_level, remap_weight):
    count, rows, levels, width = state.shape
    north_masks = [offsets[0] == offset for offset in range(-1, 3)]
    east_masks = [offsets[1] == offset for offset in range(-1, 3)]
    field = state
    for substep in range(SUBSTEPS):
        padded = extended_2(field, (("lat", 1),), 2)
        picked = jnp.zeros_like(field)
        for number, offset in enumerate(range(-1, 3)):
            picked = jnp.where(
                north_masks[number][None], padded[:, offset + 2 : offset + 2 + rows], picked
            )
        north = courant[0][None] * picked
        below = from_behind(north[:, rows - 1 :], "lat", 1)
        south = jnp.concatenate([below, north[:, : rows - 1]], axis=1)
        moved = jnp.zeros_like(field)
        for number, offset in enumerate(range(-1, 3)):
            moved = jnp.where(east_masks[number][None], jnp.roll(field, -offset, axis=3), moved)
        east = courant[1][None] * moved
        west = jnp.roll(east, 1, axis=3)
        field = field - (north - south) - (east - west)
    heating = field[0] * log_thickness
    lower_local = jnp.cumsum(heating[:, ::-1], axis=1)[:, ::-1] - heating
    column_sum = jnp.sum(heating, axis=1)
    deeper = entering(column_sum, "lev", add_terms, jnp.zeros_like(column_sum))
    geopotential = surface[:, None, :] + deeper[:, None, :] + lower_local + 0.5 * heating
    total_levels = remap_level.shape[1]
    delta_col = (remap_level - jnp.arange(total_levels, dtype=jnp.int32)[None, :, None]).astype(
        jnp.float32
    )
    inputs = lax.all_to_all(
        jnp.stack([delta_col, remap_weight]), "lev", split_axis=2, concat_axis=3, tiled=True
    )
    margin = 4
    before = []
    before.insert(0, from_behind(field, "lev", 1))
    after_list = [from_behind(field, "lev", -1)]
    joined = jnp.concatenate(before + [field] + after_list, axis=2)
    first = lax.axis_index("lev") * levels
    whole = levels * lax.axis_size("lev")
    position = first - margin + jnp.arange(levels + 2 * margin, dtype=jnp.int32)
    where_from = jnp.clip(position, 0, whole - 1) - (first - margin)
    extended = jnp.take(joined, where_from, axis=2)
    remapped = local_parabola(extended, inputs[0][None], inputs[1][None])
    return (remapped, geopotential)


MARGIN = 4
UNROLL = 3
MESH = pl.DeviceIdType.MESH


def remote(src, dst, send, recv, axis, peer):
    return pltpu.make_async_remote_copy(
        src_ref=src,
        dst_ref=dst,
        send_sem=send,
        recv_sem=recv,
        device_id={axis: peer},
        device_id_type=MESH,
    )


def compact(count):
    sizes, size = [8] * (count // 8), 4
    count %= 8
    while count:
        if count >= size:
            sizes.append(size)
            count -= size
        size //= 2
    return sizes


def kernel(lats, levs, chunks, *refs):
    (
        h_state,
        h_courant,
        h_offsets,
        h_thickness,
        h_surface,
        h_level,
        h_weight,
        out,
        geo,
        state,
        courant,
        offsets,
        thickness,
        surface,
        remap_level,
        remap_weight,
        pack_c,
        work_c,
        rpack,
        rrecv,
        rall,
        hsum,
        psum,
        csum,
        sums,
        deep,
        ins,
        fs,
        fr,
        bs,
        br,
        zs,
        zr,
        rs,
        rr,
        ps,
        pr,
        ss,
        sr,
    ) = refs[:39]
    count, rows, levels, width = state.shape
    groups = compact(count)
    parts = len(groups)
    packs, works, mids, rets, exts = (
        refs[39 + n * parts : 39 + (n + 1) * parts] for n in range(5)
    )
    slab = rows * lats
    piece = remap_level.shape[2]
    span = width // chunks
    me = lax.axis_index("lat")
    lev = lax.axis_index("lev")
    core = lax.rem(lev, 2)

    loads = [
        pltpu.make_async_copy(a, b, ins.at[n])
        for n, (a, b) in enumerate(
            (
                (h_state, state),
                (h_courant, courant),
                (h_offsets, offsets),
                (h_level, remap_level),
                (h_weight, remap_weight),
                (h_thickness, thickness),
                (h_surface, surface),
            )
        )
    ]
    for c in loads:
        c.start()
    barrier = pltpu.get_barrier_semaphore()
    for d in range(1, levs):
        pl.semaphore_signal(
            barrier, inc=1, device_id={"lev": lax.rem(lev + d, levs)}, device_id_type=MESH
        )
    for d in range(1, lats):
        pl.semaphore_signal(
            barrier, inc=1, device_id={"lat": lax.rem(me + d, lats)}, device_id_type=MESH
        )
    for c in loads[:3]:
        c.wait()
    for level in range(levels):
        at = slice(level, level + 1)
        for r in range(rows):
            f = 0
            for ref, size in zip(packs, groups):
                for g in range(size):
                    ref[level, r, g : g + 1, :] = state[f, r, at, :]
                    f += 1
            for g in range(2):
                pack_c[level, r, g : g + 1, :] = courant[g, r, at, :]
                pack_c[level, r, g + 2 : g + 3, :] = offsets[g, r, at, :].astype(jnp.float32)

    pl.semaphore_wait(barrier, lats + levs - 2)
    fwd = [[] for _ in groups]
    for g in range(parts):
        for d in range(1, lats):
            peer = lax.rem(me + d, lats)
            if g == 0:
                c = remote(
                    pack_c.at[peer],
                    work_c.at[pl.ds(1 + rows * me, rows)],
                    fs.at[parts, d],
                    fr.at[parts, d],
                    "lat",
                    peer,
                )
                c.start()
                fwd[g].append(c)
            c = remote(
                packs[g].at[peer],
                works[g].at[pl.ds(2 + rows * me, rows)],
                fs.at[g, d],
                fr.at[g, d],
                "lat",
                peer,
            )
            c.start()
            fwd[g].append(c)

    for c in loads[3:]:
        c.wait()
    first = []
    for p in range(levs):
        for r in range(rows):
            lo = p * levels
            ks = lo + lax.broadcasted_iota(jnp.int32, (levels, piece), 0)
            rpack[p, 0, r] = (remap_level[r, lo : lo + levels, :] - ks).astype(jnp.float32)
            rpack[p, 1, r] = remap_weight[r, lo : lo + levels, :]
    for d in range(1, levs):
        peer = lax.rem(lev + d, levs)
        c = remote(rpack.at[peer], rrecv.at[lev], rs.at[d], rr.at[d], "lev", peer)
        c.start()
        first.append(c)
    rrecv[lev] = rpack[lev]

    for r in range(rows):
        work_c[1 + rows * me + r] = pack_c[me, r]
        for work, ref in zip(works, packs):
            work[2 + rows * me + r] = ref[me, r]
    for work, mid in zip(works, mids):
        blank = jnp.zeros(work.shape[1:], jnp.float32)
        for r in (0, 1, slab + 2, slab + 3):
            work[r] = blank
            mid[r] = blank

    def substep(source, target, shift):
        whole = source.shape[1:]

        def face(j, south):
            q = source[j + 2]
            o0 = jnp.broadcast_to(work_c[j + 1, 2:3, :], whole)
            o1 = jnp.broadcast_to(work_c[j + 1, 3:4, :], whole)
            c0 = jnp.broadcast_to(work_c[j + 1, 0:1, :], whole)
            c1 = jnp.broadcast_to(work_c[j + 1, 1:2, :], whole)
            up = jnp.where(
                o0 < 0.5,
                jnp.where(o0 == 0.0, q, source[j + 1]),
                jnp.where(o0 == 1.0, source[j + 3], source[j + 4]),
            )
            north = c0 * up
            side = jnp.where(
                o1 < 0.5,
                jnp.where(o1 == 0.0, q, pltpu.roll(q, 1, 1)),
                jnp.where(o1 == 1.0, pltpu.roll(q, width - 1, 1), pltpu.roll(q, width - 2, 1)),
            )
            east = c1 * side
            west = pltpu.roll(east, 1, 1)
            target[j + shift] = q - (north - south) - (east - west)
            return north

        lax.fori_loop(0, slab, face, jnp.zeros(whole, jnp.float32), unroll=UNROLL)

    back = []
    for g in range(parts):
        for c in fwd[g]:
            c.wait_recv()
        substep(works[g], mids[g], 2)
        substep(mids[g], rets[g], 0)
        back.append([])
        for n in range(chunks):
            lanes = pl.ds(n * span, span)
            some = []
            for d in range(1, lats):
                peer = lax.rem(me + d, lats)
                c = remote(
                    rets[g].at[pl.ds(rows * peer, rows), :, lanes],
                    exts[g].at[MARGIN + me, :, :, lanes],
                    bs.at[n, d, g],
                    br.at[n, d, g],
                    "lat",
                    peer,
                )
                c.start()
                some.append(c)
            back[g].append(some)
    for r in range(rows):
        for ret, ext in zip(rets, exts):
            ext[MARGIN + me, r] = ret[rows * me + r]
    for c in first:
        c.wait_recv()
    for p in range(levs):
        rall[:, :, :, p * piece : (p + 1) * piece] = rrecv[p]

    def level_copy(n, way, g):
        lanes = pl.ds(n * span, span)
        source, target = ((levels, 0), (MARGIN, MARGIN + levels))[way]
        peer = (jnp.minimum(lev + 1, levs - 1), jnp.maximum(lev - 1, 0))[way]
        return remote(
            exts[g].at[pl.ds(source, MARGIN), :, :, lanes],
            exts[g].at[pl.ds(target, MARGIN), :, :, lanes],
            zs.at[n, way, g],
            zr.at[n, way, g],
            "lev",
            peer,
        )

    def pair_copy(n):
        return remote(hsum.at[n], psum.at[n], ps.at[n], pr.at[n], "lev", lev + 1 - 2 * core)

    def sum_copy(n, d):
        return remote(
            csum.at[n], sums.at[n, d], ss.at[n, d], sr.at[n, d], "lev", jnp.maximum(lev - 2 * d, core)
        )

    def heating(n, r):
        lanes = pl.ds(n * span, span)
        return [
            exts[0][MARGIN + k, r, 0:1, lanes] * thickness[r, k : k + 1, lanes]
            for k in range(levels)
        ]

    def pass_on(n):
        pair_copy(n).wait_recv()
        csum[n] = hsum[n] + psum[n]
        for d in range(1, levs // 2):

            @pl.when(lev >= 2 * d)
            def _():
                sum_copy(n, d).start()

    for g in range(parts):
        for n in range(chunks):
            for c in back[g][n]:
                c.wait_recv()
            if g == 0:
                for r in range(rows):
                    hsum[n, r] = functools.reduce(add_terms, heating(n, r))
                pair_copy(n).start()

            @pl.when(lev < levs - 1)
            def _():
                level_copy(n, 0, g).start()

            @pl.when(lev > 0)
            def _():
                level_copy(n, 1, g).start()

            if g == 0 and n > 0:
                pass_on(n - 1)
        if g == 0:
            pass_on(chunks - 1)

    def remap(g, n):
        lanes = pl.ds(n * span, span)
        ext, size, lo = exts[g], groups[g], sum(groups[:g])

        @pl.when(lev > 0)
        def _():
            level_copy(n, 0, g).wait_recv()

        @pl.when(lev < levs - 1)
        def _():
            level_copy(n, 1, g).wait_recv()

        @pl.when(lev == 0)
        def _():
            for m in range(MARGIN):
                ext[m, :, :, lanes] = ext[MARGIN, :, :, lanes]

        @pl.when(lev == levs - 1)
        def _():
            for m in range(MARGIN):
                ext[MARGIN + levels + m, :, :, lanes] = ext[MARGIN + levels - 1, :, :, lanes]

        for r in range(rows):
            q = [ext[m, r, :, lanes] for m in range(levels + 2 * MARGIN)]
            edge = {
                m: (7.0 * (q[m - 1] + q[m]) - (q[m - 2] + q[m + 1])) * (1.0 / 12.0)
                for m in range(2, levels + 2 * MARGIN - 1)
            }
            for k in range(levels):
                delta = jnp.broadcast_to(rall[0, r, k : k + 1, lanes], q[0].shape)
                weight = jnp.broadcast_to(rall[1, r, k : k + 1, lanes], q[0].shape)
                s = k + MARGIN
                centre, left, right = q[s - 2], edge[s - 2], edge[s - 1]
                for o in range(-1, 3):
                    chosen = delta == float(o)
                    centre = jnp.where(chosen, q[s + o], centre)
                    left = jnp.where(chosen, edge[s + o], left)
                    right = jnp.where(chosen, edge[s + o + 1], right)
                curve = 6.0 * centre - 3.0 * (left + right)
                value = left + weight * ((right - left) + curve * (1.0 - weight))
                for f in range(size):
                    out[lo + f, r, k : k + 1, lanes] = value[f : f + 1]

    for n in range(chunks):
        remap(0, n)

    for n in range(chunks):
        lanes = pl.ds(n * span, span)
        deep[...] = jnp.where(core == 0, psum[n], jnp.zeros_like(deep))
        for d in range(1, levs // 2):

            @pl.when(lev + 2 * d < levs)
            def _():
                sum_copy(n, d).wait_recv()
                deep[...] += sums[n, d]

        for r in range(rows):
            heat = heating(n, r)
            below = surface[r : r + 1, lanes] + deep[r]
            for k in range(levels - 1, -1, -1):
                geo[r, k : k + 1, lanes] = below + 0.5 * heat[k]
                below = below + heat[k]

    for g in range(1, parts):
        for n in range(chunks):
            remap(g, n)

    for c in sum(fwd, first):
        c.wait_send()
    for n in range(chunks):
        for g in range(parts):
            for c in back[g][n]:
                c.wait_send()
        pair_copy(n).wait_send()

        @pl.when(lev < levs - 1)
        def _():
            for g in range(parts):
                level_copy(n, 0, g).wait_send()

        @pl.when(lev > 0)
        def _():
            for g in range(parts):
                level_copy(n, 1, g).wait_send()

        for d in range(1, levs // 2):

            @pl.when(lev >= 2 * d)
            def _():
                sum_copy(n, d).wait_send()


def fused(lats, levs, chunks, *args):
    state, courant, offsets, thickness, surface, level, weight = args
    count, rows, levels, width = state.shape
    piece = level.shape[2]
    slab = rows * lats
    span = width // chunks
    f32 = jnp.float32
    dma = pltpu.SemaphoreType.DMA
    groups = compact(count)
    parts = len(groups)
    return pl.pallas_call(
        functools.partial(kernel, lats, levs, chunks),
        out_shape=(pltpu.VMEM(state.shape, f32), pltpu.VMEM(thickness.shape, f32)),
        in_specs=[pl.BlockSpec(memory_space=pl.ANY)] * 7,
        scratch_shapes=[
            *(pltpu.VMEM(x.shape, x.dtype) for x in args),
            pltpu.VMEM((levels, rows, 4, width), f32),
            pltpu.VMEM((slab + 2, 4, width), f32),
            pltpu.VMEM((levs, 2, rows, levels, piece), f32),
            pltpu.VMEM((levs, 2, rows, levels, piece), f32),
            pltpu.VMEM((2, rows, levels, width), f32),
            pltpu.VMEM((chunks, rows, 1, span), f32),
            pltpu.VMEM((chunks, rows, 1, span), f32),
            pltpu.VMEM((chunks, rows, 1, span), f32),
            pltpu.VMEM((chunks, levs // 2, rows, 1, span), f32),
            pltpu.VMEM((rows, 1, span), f32),
            dma((7,)),
            dma((parts + 1, lats)),
            dma((parts + 1, lats)),
            dma((chunks, lats, parts)),
            dma((chunks, lats, parts)),
            dma((chunks, 2, parts)),
            dma((chunks, 2, parts)),
            dma((levs,)),
            dma((levs,)),
            dma((chunks,)),
            dma((chunks,)),
            dma((chunks, levs // 2)),
            dma((chunks, levs // 2)),
            *(pltpu.VMEM((levels, rows, g, width), f32) for g in groups),
            *(pltpu.VMEM((slab + 4, g, width), f32) for g in groups),
            *(pltpu.VMEM((slab + 4, g, width), f32) for g in groups),
            *(pltpu.VMEM((slab, g, width), f32) for g in groups),
            *(pltpu.VMEM((levels + 2 * MARGIN, rows, g, width), f32) for g in groups),
        ],
        compiler_params=pltpu.CompilerParams(collective_id=0, has_side_effects=True),
    )(*args)


def solution(mesh):
    in_specs = (
        P(None, "lat", "lev", None),
        P(None, "lat", "lev", None),
        P(None, "lat", "lev", None),
        P("lat", "lev", None),
        P("lat", None),
        P("lat", None, "lev"),
        P("lat", None, "lev"),
    )
    out_specs = (P(None, "lat", "lev", None), P("lat", "lev", None))
    lats, levs = mesh.shape["lat"], mesh.shape["lev"]

    def body(state, *rest):
        levels, width = state.shape[2:]
        chunks = next((c for c in (3, 2, 1) if width % (c * 128) == 0), 0)
        if levels != lats or levels < MARGIN or chunks == 0 or levs % 2:
            return per_device(state, *rest)
        return fused(lats, levs, chunks, state, *rest)

    return jax.shard_map(
        body, mesh=mesh, in_specs=in_specs, out_specs=out_specs, check_vma=False
    )
```

```python
import functools

import jax
import jax.numpy as jnp
from jax import lax
from jax.experimental import pallas as pl
from jax.experimental.pallas import tpu as pltpu
from jax.sharding import PartitionSpec as P

SUBSTEPS = 2


def extended_2(block, sides, width):
    for axis, dim in sides:
        count = lax.axis_size(axis)
        forward = [(i, i + 1) for i in range(count - 1)]
        backward = [(target, source) for source, target in forward]
        low = lax.ppermute(
            lax.slice_in_dim(block, block.shape[dim] - width, None, axis=dim), axis, forward
        )
        high = lax.ppermute(lax.slice_in_dim(block, 0, width, axis=dim), axis, backward)
        block = jnp.concatenate([low, block, high], axis=dim)
    return block


def from_behind(x, axis, by):
    count = lax.axis_size(axis)
    pairs = [(i, i + by) for i in range(count) if 0 <= i + by < count]
    return lax.ppermute(x, axis, pairs)


def entering(x, axis, combine, identity):
    count, position = (lax.axis_size(axis), lax.axis_index(axis))
    everything = lax.all_gather(x, axis)
    start = jnp.broadcast_to(jnp.asarray(identity, x.dtype), x.shape)

    def lap(k, before):
        at = count - 1 - k
        reached = at > position
        new = combine(before, everything[at])
        return jnp.where(reached, new, before)

    return lax.fori_loop(0, count, lap, start)


def local_parabola(extended, delta, weight):
    margin = 4
    count = extended.shape[-2] - 2 * margin
    edges = (
        7.0 * (extended[..., 1:-2, :] + extended[..., 2:-1, :])
        - (extended[..., :-3, :] + extended[..., 3:, :])
    ) / 12.0
    centre = jnp.zeros(extended.shape[:-2] + (count, extended.shape[-1]), jnp.float32)
    left = centre
    right = centre
    for offset in range(-2, 3):
        chosen = delta == offset
        start = margin + offset
        centre = jnp.where(chosen, extended[..., start : start + count, :], centre)
        left = jnp.where(chosen, edges[..., start - 2 : start - 2 + count, :], left)
        right = jnp.where(chosen, edges[..., start - 1 : start - 1 + count, :], right)
    slope = right - left
    curve = 6.0 * centre - 3.0 * (left + right)
    return left + weight * (slope + curve * (1.0 - weight))


def add_terms(earlier, later):
    return earlier + later


def per_device(state, courant, offsets, log_thickness, surface, remap_level, remap_weight):
    count, rows, levels, width = state.shape
    north_masks = [offsets[0] == offset for offset in range(-1, 3)]
    east_masks = [offsets[1] == offset for offset in range(-1, 3)]
    field = state
    for substep in range(SUBSTEPS):
        padded = extended_2(field, (("lat", 1),), 2)
        picked = jnp.zeros_like(field)
        for number, offset in enumerate(range(-1, 3)):
            picked = jnp.where(
                north_masks[number][None], padded[:, offset + 2 : offset + 2 + rows], picked
            )
        north = courant[0][None] * picked
        below = from_behind(north[:, rows - 1 :], "lat", 1)
        south = jnp.concatenate([below, north[:, : rows - 1]], axis=1)
        moved = jnp.zeros_like(field)
        for number, offset in enumerate(range(-1, 3)):
            moved = jnp.where(east_masks[number][None], jnp.roll(field, -offset, axis=3), moved)
        east = courant[1][None] * moved
        west = jnp.roll(east, 1, axis=3)
        field = field - (north - south) - (east - west)
    heating = field[0] * log_thickness
    lower_local = jnp.cumsum(heating[:, ::-1], axis=1)[:, ::-1] - heating
    column_sum = jnp.sum(heating, axis=1)
    deeper = entering(column_sum, "lev", add_terms, jnp.zeros_like(column_sum))
    geopotential = surface[:, None, :] + deeper[:, None, :] + lower_local + 0.5 * heating
    total_levels = remap_level.shape[1]
    delta_col = (remap_level - jnp.arange(total_levels, dtype=jnp.int32)[None, :, None]).astype(
        jnp.float32
    )
    inputs = lax.all_to_all(
        jnp.stack([delta_col, remap_weight]), "lev", split_axis=2, concat_axis=3, tiled=True
    )
    margin = 4
    before = []
    before.insert(0, from_behind(field, "lev", 1))
    after_list = [from_behind(field, "lev", -1)]
    joined = jnp.concatenate(before + [field] + after_list, axis=2)
    first = lax.axis_index("lev") * levels
    whole = levels * lax.axis_size("lev")
    position = first - margin + jnp.arange(levels + 2 * margin, dtype=jnp.int32)
    where_from = jnp.clip(position, 0, whole - 1) - (first - margin)
    extended = jnp.take(joined, where_from, axis=2)
    remapped = local_parabola(extended, inputs[0][None], inputs[1][None])
    return (remapped, geopotential)


MARGIN = 4
UNROLL = 3
MESH = pl.DeviceIdType.MESH


def remote(src, dst, send, recv, axis, peer):
    return pltpu.make_async_remote_copy(
        src_ref=src,
        dst_ref=dst,
        send_sem=send,
        recv_sem=recv,
        device_id={axis: peer},
        device_id_type=MESH,
    )


def compact(count):
    sizes, size = [8] * (count // 8), 4
    count %= 8
    while count:
        if count >= size:
            sizes.append(size)
            count -= size
        size //= 2
    return sizes


def kernel(lats, levs, chunks, *refs):
    (
        h_state,
        h_courant,
        h_offsets,
        h_thickness,
        h_surface,
        h_level,
        h_weight,
        out,
        geo,
        state,
        courant,
        offsets,
        thickness,
        surface,
        remap_level,
        remap_weight,
        pack_c,
        work_c,
        rpack,
        rrecv,
        rall,
        hsum,
        psum,
        csum,
        sums,
        deep,
        ins,
        fs,
        fr,
        bs,
        br,
        zs,
        zr,
        rs,
        rr,
        ps,
        pr,
        ss,
        sr,
    ) = refs[:39]
    count, rows, levels, width = state.shape
    groups = compact(count)
    parts = len(groups)
    packs, works, mids, rets, exts = (
        refs[39 + n * parts : 39 + (n + 1) * parts] for n in range(5)
    )
    slab = rows * lats
    piece = remap_level.shape[2]
    span = width // chunks
    me = lax.axis_index("lat")
    lev = lax.axis_index("lev")
    core = lax.rem(lev, 2)

    loads = [
        pltpu.make_async_copy(a, b, ins.at[n])
        for n, (a, b) in enumerate(
            (
                (h_state, state),
                (h_courant, courant),
                (h_offsets, offsets),
                (h_level, remap_level),
                (h_weight, remap_weight),
                (h_thickness, thickness),
                (h_surface, surface),
            )
        )
    ]
    barrier = pltpu.get_barrier_semaphore()
    for d in range(1, levs):
        pl.semaphore_signal(
            barrier, inc=1, device_id={"lev": lax.rem(lev + d, levs)}, device_id_type=MESH
        )
    for d in range(1, lats):
        pl.semaphore_signal(
            barrier, inc=1, device_id={"lat": lax.rem(me + d, lats)}, device_id_type=MESH
        )
    for c in loads:
        c.start()
    for c in loads[:3]:
        c.wait()
    for level in range(levels):
        at = slice(level, level + 1)
        for r in range(rows):
            f = 0
            for ref, size in zip(packs, groups):
                for g in range(size):
                    ref[level, r, g : g + 1, :] = state[f, r, at, :]
                    f += 1
            for g in range(2):
                pack_c[level, r, g : g + 1, :] = courant[g, r, at, :]
                pack_c[level, r, g + 2 : g + 3, :] = offsets[g, r, at, :].astype(jnp.float32)

    for c in loads[3:]:
        c.wait()
    first = []
    for p in range(levs):
        for r in range(rows):
            lo = p * levels
            ks = lo + lax.broadcasted_iota(jnp.int32, (levels, piece), 0)
            rpack[p, 0, r] = (remap_level[r, lo : lo + levels, :] - ks).astype(jnp.float32)
            rpack[p, 1, r] = remap_weight[r, lo : lo + levels, :]
    pl.semaphore_wait(barrier, lats + levs - 2)
    fwd = [[] for _ in groups]
    for g in range(parts):
        for d in range(1, lats):
            peer = lax.rem(me + d, lats)
            if g == 0:
                c = remote(
                    pack_c.at[peer],
                    work_c.at[pl.ds(1 + rows * me, rows)],
                    fs.at[parts, d],
                    fr.at[parts, d],
                    "lat",
                    peer,
                )
                c.start()
                fwd[g].append(c)
            c = remote(
                packs[g].at[peer],
                works[g].at[pl.ds(2 + rows * me, rows)],
                fs.at[g, d],
                fr.at[g, d],
                "lat",
                peer,
            )
            c.start()
            fwd[g].append(c)

    for d in range(1, levs):
        peer = lax.rem(lev + d, levs)
        c = remote(rpack.at[peer], rrecv.at[lev], rs.at[d], rr.at[d], "lev", peer)
        c.start()
        first.append(c)
    rrecv[lev] = rpack[lev]

    for r in range(rows):
        work_c[1 + rows * me + r] = pack_c[me, r]
        for work, ref in zip(works, packs):
            work[2 + rows * me + r] = ref[me, r]
    for work, mid in zip(works, mids):
        blank = jnp.zeros(work.shape[1:], jnp.float32)
        for r in (0, 1, slab + 2, slab + 3):
            work[r] = blank
            mid[r] = blank

    def substep(source, target, shift):
        whole = source.shape[1:]

        def face(j, south):
            q = source[j + 2]
            o0 = jnp.broadcast_to(work_c[j + 1, 2:3, :], whole)
            o1 = jnp.broadcast_to(work_c[j + 1, 3:4, :], whole)
            c0 = jnp.broadcast_to(work_c[j + 1, 0:1, :], whole)
            c1 = jnp.broadcast_to(work_c[j + 1, 1:2, :], whole)
            up = jnp.where(
                o0 < 0.5,
                jnp.where(o0 == 0.0, q, source[j + 1]),
                jnp.where(o0 == 1.0, source[j + 3], source[j + 4]),
            )
            north = c0 * up
            side = jnp.where(
                o1 < 0.5,
                jnp.where(o1 == 0.0, q, pltpu.roll(q, 1, 1)),
                jnp.where(o1 == 1.0, pltpu.roll(q, width - 1, 1), pltpu.roll(q, width - 2, 1)),
            )
            east = c1 * side
            west = pltpu.roll(east, 1, 1)
            target[j + shift] = q - (north - south) - (east - west)
            return north

        lax.fori_loop(0, slab, face, jnp.zeros(whole, jnp.float32), unroll=UNROLL)

    back = []
    for g in range(parts):
        for c in fwd[g]:
            c.wait_recv()
        substep(works[g], mids[g], 2)
        substep(mids[g], rets[g], 0)
        back.append([])
        for n in range(chunks):
            lanes = pl.ds(n * span, span)
            some = []
            for d in range(1, lats):
                peer = lax.rem(me + d, lats)
                c = remote(
                    rets[g].at[pl.ds(rows * peer, rows), :, lanes],
                    exts[g].at[MARGIN + me, :, :, lanes],
                    bs.at[n, d, g],
                    br.at[n, d, g],
                    "lat",
                    peer,
                )
                c.start()
                some.append(c)
            back[g].append(some)
    for r in range(rows):
        for ret, ext in zip(rets, exts):
            ext[MARGIN + me, r] = ret[rows * me + r]
    for c in first:
        c.wait_recv()
    for p in range(levs):
        rall[:, :, :, p * piece : (p + 1) * piece] = rrecv[p]

    def level_copy(n, way, g):
        lanes = pl.ds(n * span, span)
        source, target = ((levels, 0), (MARGIN, MARGIN + levels))[way]
        peer = (jnp.minimum(lev + 1, levs - 1), jnp.maximum(lev - 1, 0))[way]
        return remote(
            exts[g].at[pl.ds(source, MARGIN), :, :, lanes],
            exts[g].at[pl.ds(target, MARGIN), :, :, lanes],
            zs.at[n, way, g],
            zr.at[n, way, g],
            "lev",
            peer,
        )

    def pair_copy(n):
        return remote(hsum.at[n], psum.at[n], ps.at[n], pr.at[n], "lev", lev + 1 - 2 * core)

    def sum_copy(n, d):
        return remote(
            csum.at[n], sums.at[n, d], ss.at[n, d], sr.at[n, d], "lev", jnp.maximum(lev - 2 * d, core)
        )

    def heating(n, r):
        lanes = pl.ds(n * span, span)
        return [
            exts[0][MARGIN + k, r, 0:1, lanes] * thickness[r, k : k + 1, lanes]
            for k in range(levels)
        ]

    def pass_on(n):
        pair_copy(n).wait_recv()
        csum[n] = hsum[n] + psum[n]
        for d in range(1, levs // 2):

            @pl.when(lev >= 2 * d)
            def _():
                sum_copy(n, d).start()

    for g in range(parts):
        for n in range(chunks):
            for c in back[g][n]:
                c.wait_recv()
            if g == 0:
                for r in range(rows):
                    hsum[n, r] = functools.reduce(add_terms, heating(n, r))
                pair_copy(n).start()

            @pl.when(lev < levs - 1)
            def _():
                level_copy(n, 0, g).start()

            @pl.when(lev > 0)
            def _():
                level_copy(n, 1, g).start()

            if g == 0 and n > 0:
                pass_on(n - 1)
        if g == 0:
            pass_on(chunks - 1)

    def remap(g, n):
        lanes = pl.ds(n * span, span)
        ext, size, lo = exts[g], groups[g], sum(groups[:g])

        @pl.when(lev > 0)
        def _():
            level_copy(n, 0, g).wait_recv()

        @pl.when(lev < levs - 1)
        def _():
            level_copy(n, 1, g).wait_recv()

        @pl.when(lev == 0)
        def _():
            for m in range(MARGIN):
                ext[m, :, :, lanes] = ext[MARGIN, :, :, lanes]

        @pl.when(lev == levs - 1)
        def _():
            for m in range(MARGIN):
                ext[MARGIN + levels + m, :, :, lanes] = ext[MARGIN + levels - 1, :, :, lanes]

        for r in range(rows):
            q = [ext[m, r, :, lanes] for m in range(levels + 2 * MARGIN)]
            edge = {
                m: (7.0 * (q[m - 1] + q[m]) - (q[m - 2] + q[m + 1])) * (1.0 / 12.0)
                for m in range(2, levels + 2 * MARGIN - 1)
            }
            for k in range(levels):
                delta = jnp.broadcast_to(rall[0, r, k : k + 1, lanes], q[0].shape)
                weight = jnp.broadcast_to(rall[1, r, k : k + 1, lanes], q[0].shape)
                s = k + MARGIN
                centre, left, right = q[s - 2], edge[s - 2], edge[s - 1]
                for o in range(-1, 3):
                    chosen = delta == float(o)
                    centre = jnp.where(chosen, q[s + o], centre)
                    left = jnp.where(chosen, edge[s + o], left)
                    right = jnp.where(chosen, edge[s + o + 1], right)
                curve = 6.0 * centre - 3.0 * (left + right)
                value = left + weight * ((right - left) + curve * (1.0 - weight))
                for f in range(size):
                    out[lo + f, r, k : k + 1, lanes] = value[f : f + 1]

    for n in range(chunks):
        remap(0, n)

    for n in range(chunks):
        lanes = pl.ds(n * span, span)
        deep[...] = jnp.where(core == 0, psum[n], jnp.zeros_like(deep))
        for d in range(1, levs // 2):

            @pl.when(lev + 2 * d < levs)
            def _():
                sum_copy(n, d).wait_recv()
                deep[...] += sums[n, d]

        for r in range(rows):
            heat = heating(n, r)
            below = surface[r : r + 1, lanes] + deep[r]
            for k in range(levels - 1, -1, -1):
                geo[r, k : k + 1, lanes] = below + 0.5 * heat[k]
                below = below + heat[k]

    for g in range(1, parts):
        for n in range(chunks):
            remap(g, n)

    for c in sum(fwd, first):
        c.wait_send()
    for n in range(chunks):
        for g in range(parts):
            for c in back[g][n]:
                c.wait_send()
        pair_copy(n).wait_send()

        @pl.when(lev < levs - 1)
        def _():
            for g in range(parts):
                level_copy(n, 0, g).wait_send()

        @pl.when(lev > 0)
        def _():
            for g in range(parts):
                level_copy(n, 1, g).wait_send()

        for d in range(1, levs // 2):

            @pl.when(lev >= 2 * d)
            def _():
                sum_copy(n, d).wait_send()


def fused(lats, levs, chunks, *args):
    state, courant, offsets, thickness, surface, level, weight = args
    count, rows, levels, width = state.shape
    piece = level.shape[2]
    slab = rows * lats
    span = width // chunks
    f32 = jnp.float32
    dma = pltpu.SemaphoreType.DMA
    groups = compact(count)
    parts = len(groups)
    return pl.pallas_call(
        functools.partial(kernel, lats, levs, chunks),
        out_shape=(pltpu.VMEM(state.shape, f32), pltpu.VMEM(thickness.shape, f32)),
        in_specs=[pl.BlockSpec(memory_space=pl.ANY)] * 7,
        scratch_shapes=[
            *(pltpu.VMEM(x.shape, x.dtype) for x in args),
            pltpu.VMEM((levels, rows, 4, width), f32),
            pltpu.VMEM((slab + 2, 4, width), f32),
            pltpu.VMEM((levs, 2, rows, levels, piece), f32),
            pltpu.VMEM((levs, 2, rows, levels, piece), f32),
            pltpu.VMEM((2, rows, levels, width), f32),
            pltpu.VMEM((chunks, rows, 1, span), f32),
            pltpu.VMEM((chunks, rows, 1, span), f32),
            pltpu.VMEM((chunks, rows, 1, span), f32),
            pltpu.VMEM((chunks, levs // 2, rows, 1, span), f32),
            pltpu.VMEM((rows, 1, span), f32),
            dma((7,)),
            dma((parts + 1, lats)),
            dma((parts + 1, lats)),
            dma((chunks, lats, parts)),
            dma((chunks, lats, parts)),
            dma((chunks, 2, parts)),
            dma((chunks, 2, parts)),
            dma((levs,)),
            dma((levs,)),
            dma((chunks,)),
            dma((chunks,)),
            dma((chunks, levs // 2)),
            dma((chunks, levs // 2)),
            *(pltpu.VMEM((levels, rows, g, width), f32) for g in groups),
            *(pltpu.VMEM((slab + 4, g, width), f32) for g in groups),
            *(pltpu.VMEM((slab + 4, g, width), f32) for g in groups),
            *(pltpu.VMEM((slab, g, width), f32) for g in groups),
            *(pltpu.VMEM((levels + 2 * MARGIN, rows, g, width), f32) for g in groups),
        ],
        compiler_params=pltpu.CompilerParams(collective_id=0, has_side_effects=True),
    )(*args)


def solution(mesh):
    in_specs = (
        P(None, "lat", "lev", None),
        P(None, "lat", "lev", None),
        P(None, "lat", "lev", None),
        P("lat", "lev", None),
        P("lat", None),
        P("lat", None, "lev"),
        P("lat", None, "lev"),
    )
    out_specs = (P(None, "lat", "lev", None), P("lat", "lev", None))
    lats, levs = mesh.shape["lat"], mesh.shape["lev"]

    def body(state, *rest):
        levels, width = state.shape[2:]
        chunks = next((c for c in (3, 2, 1) if width % (c * 128) == 0), 0)
        if levels != lats or levels < MARGIN or chunks == 0 or levs % 2:
            return per_device(state, *rest)
        return fused(lats, levs, chunks, state, *rest)

    return jax.shard_map(
        body, mesh=mesh, in_specs=in_specs, out_specs=out_specs, check_vma=False
    )
```
